32 devices in a mesh: rep: 2 (over core), space: 16 (over z, y, x).
Axes of the slice: x: 2, y: 2, z: 4, core: 2. Of those that a mesh axis runs over, the one named last changes fastest.
Arguments:
- particles: float32 [6, 2, 8192, 128], P(None, 'rep', 'space'), may hold values from -6 to 6
- pair_order: int32 [2, 8192, 128], P('rep', 'space'), may hold values from 0 to 127, each once within a row
- accepted: int32 [2, 8192, 64], P('rep', 'space'), may hold values 0 or 1
- direction: int32 [2, 8192, 64], P('rep', 'space'), may hold values from 0 to 255
- destination: int32 [2, 8192], P('rep', 'space'), may hold values from 0 to 15, as said below
- live_count: int32 [2, 16], P('rep', 'space'), may hold values from 256 to 512, as said below
- cell_index: int32 [2, 8192], P('rep', 'space'), may hold values from 0 to 255
Outputs:
- moved: float32 [6, 2, 12288, 128], P(None, 'rep', 'space')
- samples: float32 [4, 16, 256], P(None, 'space', 'rep')
The draws below stay inside these ranges and needn't reach their ends.
Inputs may be any that keep to these rules, and one draw needn't show every extreme that they name: Every block's destination is its own slab or one of the two beside it, slab 0 and slab 16 - 1 being beside each other; only live blocks leave; one slab of one replica sends at most 128 blocks to each of its two neighbours, and in every replica some slab sends exactly 128 to its upper and some slab exactly 128 to its lower neighbour. `live_count`: the count of live blocks of each slab of each replica; slab 0 of replica 0 is full.
All inputs are finite; a program needn't handle non-finite values. No bound on the sum of `accepted` on one device may be relied on, other than what follows from the above.
Results may differ from the reference program's by a relative error of at most 0.0003.
Values sent between devices are 32-bit elements; how exact they have to be, the bound alone decides.
A program may use at most 64 MiB of HBM per device.

```python
import jax
import jax.numpy as jnp
from jax import lax

PART = 128
PAIRS = 64
NDIR = 256
CAP = 512
MOVE = 128
CELLS = 256
OUTCAP = 768
REPS = 2
SLABS = 16
BLOCKS = 8192


def migration_plan(key):
    count_key = jax.random.fold_in(key, 101)
    upper_key = jax.random.fold_in(key, 102)
    upper_full = jax.random.fold_in(key, 103)
    lower_key = jax.random.fold_in(key, 104)
    lower_full = jax.random.fold_in(key, 105)
    order_key = jax.random.fold_in(key, 106)
    slab_ids = jnp.arange(SLABS, dtype=jnp.int32)[None, :]
    replica_ids = jnp.arange(REPS, dtype=jnp.int32)[:, None]
    living = jax.random.randint(count_key, (REPS, SLABS), CAP // 2, CAP + 1)
    living = jnp.where((slab_ids == 0) & (replica_ids == 0), CAP, living)
    upward = jax.random.randint(upper_key, (REPS, SLABS), 0, MOVE + 1)
    upward = jnp.where(slab_ids == jax.random.randint(upper_full, (REPS, 1), 0, SLABS), MOVE, upward)
    downward = jax.random.randint(lower_key, (REPS, SLABS), 0, MOVE + 1)
    downward = jnp.where(slab_ids == jax.random.randint(lower_full, (REPS, 1), 0, SLABS), MOVE, downward)
    slots = jnp.arange(CAP, dtype=jnp.int32)[None, None, :]
    noise = jax.random.randint(order_key, (REPS, SLABS, CAP), 0, 2 ** 18)
    priority = noise * CAP + slots + jnp.where(slots < living[:, :, None], 0, 2 ** 30)
    ranking = jnp.argsort(jnp.argsort(priority, axis=-1), axis=-1)
    offset = jnp.where(ranking < upward[:, :, None], 1, jnp.where(ranking < (upward + downward)[:, :, None], SLABS - 1, 0))
    target = (slab_ids[:, :, None] + offset) % SLABS
    return (living.astype(jnp.int32), target.reshape(REPS, SLABS * CAP).astype(jnp.int32))


def draw_destination(key, part):
    return migration_plan(key)[1]


def draw_live_count(key, part):
    return migration_plan(key)[0]


def place_ends(values, own_key, smallest, largest):
    index_at = [jax.random.randint(jax.random.fold_in(own_key, axis), (), 0, length) for axis, length in enumerate(values.shape)]
    widest = values.shape.index(max(values.shape))
    beside = index_at[:widest] + [(index_at[widest] + 1) % values.shape[widest]] + index_at[widest + 1:]
    return values.at[tuple(index_at)].set(smallest).at[tuple(beside)].set(largest)


def block_scale(stream_key, shape, split, least, largest):
    def one(axis_at, shards_of):
        steps = jax.random.uniform(jax.random.fold_in(jax.random.fold_in(stream_key, 6), axis_at), (shards_of,), jnp.float32, least / len(split), largest / len(split))
        return jnp.repeat(jnp.exp(steps), shape[axis_at] // shards_of).reshape((-1,) + (1,) * (len(shape) - axis_at - 1))

    level = one(*split[0])
    for cut in split[1:]:
        level = level * one(*cut)
    return level


def bell_draw(key, shape, spread, most, pieces=(), held_as=jnp.bfloat16):
    factor_of = block_scale(key, shape, pieces, -0.22, 0.18) if pieces else 1.0
    array = jax.random.normal(key, shape, jnp.float32) * spread * factor_of
    return jnp.minimum(jnp.maximum(array, -most), most).astype(held_as)


def setup_inputs(seed: int = 0) -> dict:
    keys = jax.random.split(jax.random.key(seed), 8)
    return {
        "particles": bell_draw(keys[0], (6, REPS, BLOCKS, PART), 1.0, 6.0, ((1, 2), (2, 16)), jnp.float32),
        "pair_order": jax.vmap(lambda own: jax.random.permutation(own, PART))(jax.random.split(keys[1], REPS * BLOCKS)).reshape((REPS, BLOCKS, PART)).astype(jnp.int32),
        "accepted": place_ends((jax.random.randint(keys[2], (REPS, BLOCKS, PAIRS), 0, 2) < 1).astype(jnp.int32), jax.random.fold_in(keys[2], 1), 0, 1),
        "direction": place_ends(jax.random.randint(keys[3], (REPS, BLOCKS, PAIRS), 0, NDIR), jax.random.fold_in(keys[3], 1), 0, NDIR - 1).astype(jnp.int32),
        "destination": draw_destination(jax.random.fold_in(keys[7], 71), 0),
        "live_count": draw_live_count(jax.random.fold_in(keys[7], 71), 0),
        "cell_index": place_ends(jax.random.randint(keys[6], (REPS, BLOCKS), 0, CELLS), jax.random.fold_in(keys[6], 1), 0, CELLS - 1).astype(jnp.int32),
    }


time_step = 0.25
golden_turn = 2.399963229728653

def directions(index):
    turns = index.astype(jnp.float32)
    height = 1.0 - (2.0 * turns + 1.0) / NDIR
    radius = jnp.sqrt(1.0 - height * height)
    angle = turns * golden_turn
    return jnp.stack([radius * jnp.cos(angle), radius * jnp.sin(angle), height])

def place_block(values, order):
    return jnp.zeros_like(values).at[:, order].set(values)

def collide(velocity, pair_order, accepted, direction):
    permuted = jnp.take_along_axis(velocity, pair_order[None], axis=2)
    first = permuted[:, :, :PAIRS]
    second = permuted[:, :, PAIRS:]
    center = 0.5 * (first + second)
    relative = first - second
    speed = jnp.sqrt(lax.optimization_barrier(jnp.sum(relative * relative, axis=0)))
    unit = directions(direction)
    taken = (accepted == 1)[None]
    first_out = jnp.where(taken, center + 0.5 * speed * unit, first)
    second_out = jnp.where(taken, center - 0.5 * speed * unit, second)
    combined = jnp.concatenate([first_out, second_out], axis=2)
    return jax.vmap(place_block, in_axes=(1, 0), out_axes=1)(combined, pair_order)

def moments(velocity, living):
    sums = jnp.stack([lax.optimization_barrier(jnp.sum(velocity[0], axis=1)), lax.optimization_barrier(jnp.sum(velocity[1], axis=1)), lax.optimization_barrier(jnp.sum(velocity[2], axis=1)), lax.optimization_barrier(jnp.sum(lax.optimization_barrier(jnp.sum(velocity * velocity, axis=0)), axis=1))])
    return jnp.where(living[None], sums, 0.0)

def select_movers(updated, moving):
    ranking = jnp.cumsum(moving.astype(jnp.int32)) - 1
    slots = jnp.arange(MOVE, dtype=jnp.int32)
    matches = moving[None, :] & (ranking[None, :] == slots[:, None])
    sources = jnp.arange(moving.shape[0], dtype=jnp.int32)
    chosen = lax.optimization_barrier(jnp.sum(jnp.where(matches, sources[None, :], 0), axis=1)).astype(jnp.int32)
    is_valid = jnp.any(matches, axis=1)
    return jnp.where(is_valid[None, :, None], jnp.take(updated, chosen, axis=1), 0.0)

def one_replica(inputs):
    particles, pair_order, accepted, direction, destination, live_count, cell_index = inputs
    velocity = collide(particles[3:], pair_order, accepted, direction)
    position = particles[:3] + time_step * velocity
    updated = jnp.concatenate([position, velocity], axis=0)
    block_ids = jnp.arange(BLOCKS, dtype=jnp.int32)
    slot_index = block_ids % CAP
    slab_index = block_ids // CAP
    living = slot_index < live_count[slab_index]
    to_upper = living & (destination == (slab_index + 1) % SLABS)
    to_lower = living & (destination == (slab_index + SLABS - 1) % SLABS)
    staying = living & (destination == slab_index)
    term = moments(velocity, living)
    sampled = jax.ops.segment_sum(term.T, slab_index * CELLS + cell_index, num_segments=SLABS * CELLS)
    by_slab = updated.reshape(6, SLABS, CAP, PART)
    send_upper = jax.vmap(select_movers, in_axes=(1, 0), out_axes=1)(by_slab, to_upper.reshape(SLABS, CAP))
    send_lower = jax.vmap(select_movers, in_axes=(1, 0), out_axes=1)(by_slab, to_lower.reshape(SLABS, CAP))
    from_lower = jnp.roll(send_upper, 1, axis=1)
    from_upper = jnp.roll(send_lower, -1, axis=1)
    own_blocks = jnp.where(staying.reshape(SLABS, CAP)[None, :, :, None], by_slab, 0.0)
    moved = jnp.concatenate([from_lower, own_blocks, from_upper], axis=2).reshape(6, SLABS * OUTCAP, PART)
    return (moved, sampled.T)

def reference(particles, pair_order, accepted, direction, destination, live_count, cell_index):
    inputs = (jnp.moveaxis(particles, 1, 0), pair_order, accepted, direction, destination, live_count, cell_index)
    moved, sampled = lax.map(one_replica, inputs)
    moved = jnp.moveaxis(moved, 0, 1)
    samples = (lax.optimization_barrier(jnp.sum(sampled, axis=0)) / (PART * REPS)).reshape(4, SLABS, CELLS)
    return (moved, samples)
```

```python
import functools

import jax
import jax.numpy as jnp
from jax import lax
from jax.experimental import pallas as pl
from jax.experimental.pallas import tpu as pltpu
from jax.sharding import PartitionSpec as P

NDIR = 256
MOVE = 128
CELLS = 256
TIME_STEP = 0.25
GOLDEN_TURN = 2.399963229728653
ROWS = 32


def take_lanes(values, index):
    return jnp.take_along_axis(values, index, axis=1, mode="promise_in_bounds")


def split3(value):
    high = value.astype(jnp.bfloat16)
    rest = value - high.astype(jnp.float32)
    middle = rest.astype(jnp.bfloat16)
    low = (rest - middle.astype(jnp.float32)).astype(jnp.bfloat16)
    return high, middle, low


def dot(left, right):
    return jnp.dot(left, right, preferred_element_type=jnp.float32)


def dot_nt(left, right):
    return lax.dot_general(left, right, (((1,), (1,)), ((), ())), preferred_element_type=jnp.float32)


def inverse_order(order, lane):
    part = order.shape[1]
    key = (order * part + lane).astype(jnp.float32)
    size = 2
    while size <= part:
        stride = size // 2
        while stride >= 1:
            partner = take_lanes(key, lane ^ stride)
            keep_low = ((lane & stride) == 0) == ((lane & size) == 0)
            key = jnp.where(keep_low, jnp.minimum(key, partner), jnp.maximum(key, partner))
            stride //= 2
        size *= 2
    return key.astype(jnp.int32) - lane * part


def main_kernel(slabs, part_ref, order_ref, flag_ref, turn_ref, dest_ref, live_ref, cell_ref,
                moved_ref, up_ref, down_ref, cells_ref, table, packed_t, keep_t, parts, square):
    step = pl.program_id(0)
    steps = pl.num_programs(0)
    chunk, part = order_ref.shape
    pairs = part // 2
    cap = dest_ref.shape[1]
    my_slab = lax.axis_index("space")
    upper_slab = lax.rem(my_slab + 1, slabs)
    lower_slab = lax.rem(my_slab + slabs - 1, slabs)

    @pl.when(step == 0)
    def _():
        for half in range(2):
            turns = (lax.broadcasted_iota(jnp.int32, (8, part), 1) + half * part).astype(jnp.float32)
            height = 1.0 - (2.0 * turns + 1.0) / NDIR
            radius = jnp.sqrt(1.0 - height * height)
            angle = turns * GOLDEN_TURN
            table[half] = radius * jnp.cos(angle)
            table[half + 2] = radius * jnp.sin(angle)

    pair_code = turn_ref[...] + NDIR * flag_ref[...]
    packed_t[...] = jnp.transpose(jnp.concatenate([pair_code, pair_code], axis=0))
    start = pl.multiple_of(step * chunk, chunk)
    slots = lax.broadcasted_iota(jnp.int32, (1, chunk), 1) + step * chunk
    staying = (dest_ref[:, pl.ds(start, chunk)] == my_slab) & (slots < live_ref[0, 0])
    stay_rows = jnp.broadcast_to(jnp.where(staying, 1.0, 0.0), (part, chunk))
    keep_t[...] = jnp.transpose(stay_rows)

    def rows_step(i, carry):
        row = pl.multiple_of(i * ROWS, ROWS)
        here = pl.ds(row, ROWS)
        lane = lax.broadcasted_iota(jnp.int32, (ROWS, part), 1)
        order = order_ref[here, :]
        inverse = inverse_order(order, lane)
        partner = take_lanes(order, inverse ^ pairs)
        code = take_lanes(packed_t[here, :], inverse & (pairs - 1))
        taken = code >= NDIR
        turn = code & (NDIR - 1)
        low_index = turn & (part - 1)
        is_high = turn >= part
        wide = (ROWS, part)
        tables = [jnp.broadcast_to(table[k, 0:1, :], wide) for k in range(4)]
        unit_x = jnp.where(is_high, take_lanes(tables[1], low_index), take_lanes(tables[0], low_index))
        unit_y = jnp.where(is_high, take_lanes(tables[3], low_index), take_lanes(tables[2], low_index))
        unit_z = 1.0 - (2.0 * turn.astype(jnp.float32) + 1.0) / NDIR
        old = [part_ref[3 + k, here, :] for k in range(3)]
        other = [take_lanes(v, partner) for v in old]
        relative = [a - b for a, b in zip(old, other)]
        speed = jnp.sqrt(relative[0] * relative[0] + relative[1] * relative[1] + relative[2] * relative[2])
        half_speed = jnp.where(inverse < pairs, 0.5, -0.5) * speed
        new = [
            jnp.where(taken, 0.5 * (a + b) + half_speed * u, a)
            for a, b, u in zip(old, other, (unit_x, unit_y, unit_z))
        ]
        keep = keep_t[here, :] > 0.0
        block = pl.ds(pl.multiple_of(step * chunk + row, ROWS), ROWS)
        square[block, :] = new[0] * new[0] + new[1] * new[1] + new[2] * new[2]
        moving = [part_ref[k, here, :] + TIME_STEP * new[k] for k in range(3)]
        for k, value in enumerate(moving + new):
            moved_ref[k, here, :] = jnp.where(keep, value, 0.0)
            for j, piece in enumerate(split3(value)):
                parts[j, block, pl.ds(k * part, part)] = piece
        return carry

    lax.fori_loop(0, chunk // ROWS, rows_step, 0)

    @pl.when(step == steps - 1)
    def _():
        all_slots = lax.broadcasted_iota(jnp.int32, (1, cap), 1)
        living = all_slots < live_ref[0, 0]
        to_upper = living & (dest_ref[...] == upper_slab)
        to_lower = living & (dest_ref[...] == lower_slab)
        eight = lax.broadcasted_iota(jnp.int32, (8, cap), 0)
        both = jnp.where(eight == 0, jnp.where(to_upper, 1.0, 0.0), jnp.where(to_lower, 1.0, 0.0))
        triangle = (
            lax.broadcasted_iota(jnp.int32, (cap, cap), 0) <= lax.broadcasted_iota(jnp.int32, (cap, cap), 1)
        )
        ranking = dot(both.astype(jnp.bfloat16), jnp.where(triangle, 1.0, 0.0).astype(jnp.bfloat16))
        ranking = ranking.astype(jnp.int32) - 1
        up_slot = jnp.where(to_upper, ranking[0:1, :], -1)
        down_slot = jnp.where(to_lower, ranking[1:2, :], -1)
        slot = lax.broadcasted_iota(jnp.int32, (MOVE, cap), 0)
        chosen = jnp.concatenate(
            [jnp.where(slot == up_slot, 1.0, 0.0), jnp.where(slot == down_slot, 1.0, 0.0)], axis=0
        ).astype(jnp.bfloat16)
        for k in range(0, 6, 2):
            here = pl.ds(k * part, 2 * part)
            sent = dot(chosen, parts[0, :, here]) + dot(chosen, parts[1, :, here]) + dot(chosen, parts[2, :, here])
            for j in range(2):
                up_ref[k + j] = sent[:MOVE, j * part:(j + 1) * part]
                down_ref[k + j] = sent[MOVE:, j * part:(j + 1) * part]

        ones = jnp.ones((8, part), jnp.bfloat16)
        terms = []
        for k in range(3):
            here = pl.ds((3 + k) * part, part)
            terms.append(dot_nt(ones, parts[0, :, here]) + dot_nt(ones, parts[1, :, here]) + dot_nt(ones, parts[2, :, here]))
        pieces = split3(square[...])
        terms.append(dot_nt(ones, pieces[0]) + dot_nt(ones, pieces[1]) + dot_nt(ones, pieces[2]))
        term = jnp.where(eight == 0, terms[0], jnp.where(eight == 1, terms[1], jnp.where(eight == 2, terms[2], terms[3])))
        term = jnp.where(living, term, 0.0)
        cells = lax.broadcasted_iota(jnp.int32, (CELLS, cap), 0)
        in_cell = jnp.where(cells == cell_ref[...], 1.0, 0.0).astype(jnp.bfloat16)
        high, middle, low = split3(term)
        total = dot_nt(high, in_cell) + dot_nt(middle, in_cell) + dot_nt(low, in_cell)
        cells_ref[...] = total[0:4, :]


def from_behind(value, axis, steps):
    count = lax.axis_size(axis)
    pairs = [(source, (source + steps) % count) for source in range(count)]
    return lax.ppermute(value, axis, pairs)


def per_device(particles, pair_order, accepted, direction, destination, live_count, cell_index):
    six, _, cap, part = particles.shape
    pairs = accepted.shape[2]
    chunk = MOVE
    steps = cap // chunk
    slabs = lax.axis_size("space")
    reps = lax.axis_size("rep")
    f32 = jnp.float32
    out_cap = cap + 2 * MOVE
    moved, send_upper, send_lower, cell_terms = pl.pallas_call(
        functools.partial(main_kernel, slabs),
        grid=(steps,),
        in_specs=[
            pl.BlockSpec((six, chunk, part), lambda i: (0, i, 0)),
            pl.BlockSpec((chunk, part), lambda i: (i, 0)),
            pl.BlockSpec((pairs, chunk), lambda i: (0, i)),
            pl.BlockSpec((pairs, chunk), lambda i: (0, i)),
            pl.BlockSpec((1, cap), lambda i: (0, 0)),
            pl.BlockSpec(memory_space=pltpu.SMEM),
            pl.BlockSpec((1, cap), lambda i: (0, 0)),
        ],
        out_specs=[
            pl.BlockSpec((six, chunk, part), lambda i: (0, i + 1, 0)),
            pl.BlockSpec((six, MOVE, part), lambda i: (0, 0, 0)),
            pl.BlockSpec((six, MOVE, part), lambda i: (0, 0, 0)),
            pl.BlockSpec((4, CELLS), lambda i: (0, 0)),
        ],
        out_shape=[
            jax.ShapeDtypeStruct((six, out_cap, part), f32),
            jax.ShapeDtypeStruct((six, MOVE, part), f32),
            jax.ShapeDtypeStruct((six, MOVE, part), f32),
            jax.ShapeDtypeStruct((4, CELLS), f32),
        ],
        scratch_shapes=[
            pltpu.VMEM((4, 8, part), f32),
            pltpu.VMEM((chunk, part), jnp.int32),
            pltpu.VMEM((chunk, part), f32),
            pltpu.VMEM((3, cap, six * part), jnp.bfloat16),
            pltpu.VMEM((cap, part), f32),
        ],
        name="step",
    )(
        particles.reshape(six, cap, part),
        pair_order.reshape(cap, part),
        jnp.transpose(accepted.reshape(cap, pairs)),
        jnp.transpose(direction.reshape(cap, pairs)),
        destination.reshape(1, cap),
        live_count,
        cell_index.reshape(1, cap),
    )
    from_lower = from_behind(send_upper, "space", 1)
    from_upper = from_behind(send_lower, "space", -1)
    share = CELLS // reps
    my_rep = lax.axis_index("rep")
    total = lax.dynamic_slice_in_dim(cell_terms, my_rep * share, share, 1)
    for away in range(1, reps):
        theirs = lax.rem(my_rep + away, reps)
        outgoing = lax.dynamic_slice_in_dim(cell_terms, theirs * share, share, 1)
        total = total + from_behind(outgoing, "rep", away)
    samples = (total / (part * reps))[:, None, :]
    moved = lax.dynamic_update_slice(moved, from_lower, (0, 0, 0))
    moved = lax.dynamic_update_slice(moved, from_upper, (0, MOVE + cap, 0))
    return (moved[:, None], samples)


def solution(mesh):
    return jax.shard_map(
        per_device,
        mesh=mesh,
        in_specs=(
            P(None, "rep", "space", None),
            P("rep", "space", None),
            P("rep", "space", None),
            P("rep", "space", None),
            P("rep", "space"),
            P("rep", "space"),
            P("rep", "space"),
        ),
        out_specs=(P(None, "rep", "space", None), P(None, "space", "rep")),
        check_vma=False,
    )
```

```python
import functools

import jax
import jax.numpy as jnp
from jax import lax
from jax.experimental import pallas as pl
from jax.experimental.pallas import tpu as pltpu
from jax.sharding import PartitionSpec as P


NDIR = 256
MOVE = 128
CELLS = 256
TIME_STEP = 0.25
GOLDEN_TURN = 2.399963229728653
ROWS = 128


def take_lanes(values, index):
    return jnp.take_along_axis(values, index, axis=1, mode="promise_in_bounds")


def split3(value):
    high = value.astype(jnp.bfloat16)
    rest = value - high.astype(jnp.float32)
    middle = rest.astype(jnp.bfloat16)
    low = (rest - middle.astype(jnp.float32)).astype(jnp.bfloat16)
    return high, middle, low


def dot(left, right):
    return jnp.dot(left, right, preferred_element_type=jnp.float32)


def dot_nt(left, right):
    return lax.dot_general(left, right, (((1,), (1,)), ((), ())), preferred_element_type=jnp.float32)


def inverse_order(order):
    chunk, part = order.shape
    count = part // 8
    lane = lax.broadcasted_iota(jnp.int32, (chunk, part), 1)
    keys = jnp.transpose((order * part + lane).astype(jnp.float32))
    rows = [keys[8 * i:8 * i + 8] for i in range(count)]
    sublane = lax.broadcasted_iota(jnp.int32, (8, chunk), 0)
    sign = None
    size = 2
    while size <= part:
        wanted = None
        if count <= size < part:
            wanted = jnp.where((sublane & (size // count)) == 0, 1.0, -1.0)
        if sign is not None or wanted is not None:
            flip = wanted if sign is None else sign if wanted is None else sign * wanted
            rows = [row * flip for row in rows]
        sign = wanted
        stride = size // 2
        while stride >= 1:
            if stride >= count:
                apart = stride // count
                is_low = (sublane & apart) == 0
                swapped = [jnp.take_along_axis(row, sublane ^ apart, axis=0, mode="promise_in_bounds") for row in rows]
                rows = [jnp.where(is_low, jnp.minimum(r, o), jnp.maximum(r, o)) for r, o in zip(rows, swapped)]
            else:
                after = list(rows)
                for i in range(count):
                    j = i ^ stride
                    rising = size >= count or (i & size) == 0
                    pick = jnp.minimum if (i < j) == rising else jnp.maximum
                    after[i] = pick(rows[i], rows[j])
                rows = after
            stride //= 2
        size *= 2
    ranked = [(row - ((sublane * count + i) * part).astype(jnp.float32)) for i, row in enumerate(rows)]
    placed = jnp.transpose(jnp.concatenate(ranked, axis=0)).astype(jnp.int32)
    return take_lanes(placed, (lane & (count - 1)) * 8 + lane // count)


def pick_rows(chosen, pieces):
    return dot(chosen, pieces[0]) + dot(chosen, pieces[1]) + dot(chosen, pieces[2])


def one_hot_rows(slots, cap):
    slot = lax.broadcasted_iota(jnp.int32, (MOVE, cap), 0)
    return jnp.concatenate(
        [jnp.where(slot == slots[j:j + 1, :], 1.0, 0.0) for j in range(2)], axis=0
    ).astype(jnp.bfloat16)


def first_kernel(slabs, part_ref, dest_ref, live_ref, up_ref, down_ref, slot_ref):
    cap = dest_ref.shape[1]
    chunk = MOVE
    my_slab = lax.axis_index("space")
    upper_slab = lax.rem(my_slab + 1, slabs)
    lower_slab = lax.rem(my_slab + slabs - 1, slabs)
    living = lax.broadcasted_iota(jnp.int32, (1, cap), 1) < live_ref[0, 0]
    leaving = [living & (dest_ref[...] == upper_slab), living & (dest_ref[...] == lower_slab)]
    flags = jnp.concatenate([jnp.where(m, 1.0, 0.0) for m in leaving], axis=0)
    triangle = (
        lax.broadcasted_iota(jnp.int32, (chunk, chunk), 0) <= lax.broadcasted_iota(jnp.int32, (chunk, chunk), 1)
    )
    triangle = jnp.where(triangle, 1.0, 0.0).astype(jnp.bfloat16)
    before = jnp.zeros((2, 1), jnp.float32)
    ranks = []
    for i in range(cap // chunk):
        piece = flags[:, i * chunk:(i + 1) * chunk]
        inside = dot(piece.astype(jnp.bfloat16), triangle)
        ranks.append(inside + before)
        before = before + inside[:, chunk - 1:chunk]
    ranking = jnp.concatenate(ranks, axis=1)
    slots = jnp.where(flags > 0.0, ranking - 1.0, -1.0).astype(jnp.int32)
    slot_ref[...] = slots
    chosen = one_hot_rows(slots, cap)
    for k in range(3):
        sent = pick_rows(chosen, split3(part_ref[k]))
        up_ref[k] = sent[:MOVE]
        down_ref[k] = sent[MOVE:]


def main_kernel(part_ref, order_ref, flag_ref, turn_ref, dest_ref, live_ref, cell_ref, slot_ref,
                moved_ref, up_ref, down_ref, cells_ref, table, packed_t, keep_t, inverse_t, parts, square):
    step = pl.program_id(0)
    steps = pl.num_programs(0)
    chunk, part = order_ref.shape
    pairs = part // 2
    cap = dest_ref.shape[1]
    reps, _, share = cells_ref.shape
    my_slab = lax.axis_index("space")

    @pl.when(step == 0)
    def _():
        for half in range(2):
            turns = (lax.broadcasted_iota(jnp.int32, (8, part), 1) + half * part).astype(jnp.float32)
            height = 1.0 - (2.0 * turns + 1.0) / NDIR
            radius = jnp.sqrt(1.0 - height * height)
            angle = turns * GOLDEN_TURN
            table[half] = radius * jnp.cos(angle)
            table[half + 2] = radius * jnp.sin(angle)

    pair_code = turn_ref[...] + NDIR * flag_ref[...]
    packed_t[...] = jnp.transpose(jnp.concatenate([pair_code, pair_code], axis=0))
    start = pl.multiple_of(step * chunk, chunk)
    slots = lax.broadcasted_iota(jnp.int32, (1, chunk), 1) + step * chunk
    staying = (dest_ref[:, pl.ds(start, chunk)] == my_slab) & (slots < live_ref[0, 0])
    stay_rows = jnp.broadcast_to(jnp.where(staying, 1.0, 0.0), (part, chunk))
    keep_t[...] = jnp.transpose(stay_rows)
    inverse_t[...] = inverse_order(order_ref[...])

    def rows_step(i, carry):
        row = pl.multiple_of(i * ROWS, ROWS)
        here = pl.ds(row, ROWS)
        order = order_ref[here, :]
        inverse = inverse_t[here, :]
        partner = take_lanes(order, inverse ^ pairs)
        code = take_lanes(packed_t[here, :], inverse & (pairs - 1))
        taken = code >= NDIR
        turn = code & (NDIR - 1)
        low_index = turn & (part - 1)
        is_high = turn >= part
        wide = (ROWS, part)
        tables = [jnp.broadcast_to(table[k, 0:1, :], wide) for k in range(4)]
        unit_x = jnp.where(is_high, take_lanes(tables[1], low_index), take_lanes(tables[0], low_index))
        unit_y = jnp.where(is_high, take_lanes(tables[3], low_index), take_lanes(tables[2], low_index))
        unit_z = 1.0 - (2.0 * turn.astype(jnp.float32) + 1.0) / NDIR
        old = [part_ref[3 + k, here, :] for k in range(3)]
        other = [take_lanes(v, partner) for v in old]
        relative = [a - b for a, b in zip(old, other)]
        speed = jnp.sqrt(relative[0] * relative[0] + relative[1] * relative[1] + relative[2] * relative[2])
        half_speed = jnp.where(inverse < pairs, 0.5, -0.5) * speed
        new = [
            jnp.where(taken, 0.5 * (a + b) + half_speed * u, a)
            for a, b, u in zip(old, other, (unit_x, unit_y, unit_z))
        ]
        keep = keep_t[here, :] > 0.0
        block = pl.ds(pl.multiple_of(step * chunk + row, ROWS), ROWS)
        square[block, :] = new[0] * new[0] + new[1] * new[1] + new[2] * new[2]
        for k in range(3):
            moved_ref[k, here, :] = jnp.where(keep, part_ref[k, here, :] + TIME_STEP * new[k], 0.0)
            moved_ref[3 + k, here, :] = jnp.where(keep, new[k], 0.0)
            for j, piece in enumerate(split3(new[k])):
                parts[j, block, pl.ds(k * part, part)] = piece
        return carry

    lax.fori_loop(0, chunk // ROWS, rows_step, 0)

    @pl.when(step == steps - 1)
    def _():
        chosen = one_hot_rows(slot_ref[...], cap)
        for k in range(3):
            sent = pick_rows(chosen, [parts[j, :, pl.ds(k * part, part)] for j in range(3)])
            up_ref[k] = sent[:MOVE]
            down_ref[k] = sent[MOVE:]

        living = lax.broadcasted_iota(jnp.int32, (1, cap), 1) < live_ref[0, 0]
        ones = jnp.ones((8, part), jnp.bfloat16)
        eight = lax.broadcasted_iota(jnp.int32, (8, cap), 0)
        terms = []
        for k in range(3):
            here = pl.ds(k * part, part)
            terms.append(dot_nt(ones, parts[0, :, here]) + dot_nt(ones, parts[1, :, here]) + dot_nt(ones, parts[2, :, here]))
        pieces = split3(square[...])
        terms.append(dot_nt(ones, pieces[0]) + dot_nt(ones, pieces[1]) + dot_nt(ones, pieces[2]))
        term = jnp.where(eight == 0, terms[0], jnp.where(eight == 1, terms[1], jnp.where(eight == 2, terms[2], terms[3])))
        term = jnp.where(living, term, 0.0)
        shifted = cell_ref[...] + (CELLS - lax.axis_index("rep") * share)
        shifted = jnp.where(shifted >= CELLS, shifted - CELLS, shifted)
        cells = lax.broadcasted_iota(jnp.int32, (CELLS, cap), 0)
        in_cell = jnp.where(cells == shifted, 1.0, 0.0).astype(jnp.bfloat16)
        high, middle, low = split3(term)
        total = dot_nt(high, in_cell) + dot_nt(middle, in_cell) + dot_nt(low, in_cell)
        for j in range(reps):
            cells_ref[j] = total[0:4, j * share:(j + 1) * share]


def from_behind(value, axis, steps):
    count = lax.axis_size(axis)
    pairs = [(source, (source + steps) % count) for source in range(count)]
    return lax.ppermute(value, axis, pairs)


def per_device(particles, pair_order, accepted, direction, destination, live_count, cell_index):
    six, _, cap, part = particles.shape
    three = six // 2
    pairs = accepted.shape[2]
    chunk = MOVE
    steps = cap // chunk
    slabs = lax.axis_size("space")
    reps = lax.axis_size("rep")
    share = CELLS // reps
    f32 = jnp.float32
    out_cap = cap + 2 * MOVE
    current = particles.reshape(six, cap, part)
    targets = destination.reshape(1, cap)
    parcel = jax.ShapeDtypeStruct((three, MOVE, part), f32)
    up_position, down_position, slots = pl.pallas_call(
        functools.partial(first_kernel, slabs),
        grid=(1,),
        in_specs=[
            pl.BlockSpec((three, cap, part), lambda i: (0, 0, 0)),
            pl.BlockSpec((1, cap), lambda i: (0, 0)),
            pl.BlockSpec(memory_space=pltpu.SMEM),
        ],
        out_specs=[
            pl.BlockSpec((three, MOVE, part), lambda i: (0, 0, 0)),
            pl.BlockSpec((three, MOVE, part), lambda i: (0, 0, 0)),
            pl.BlockSpec((2, cap), lambda i: (0, 0)),
        ],
        out_shape=[parcel, parcel, jax.ShapeDtypeStruct((2, cap), jnp.int32)],
        name="first",
    )(current, targets, live_count)
    lower_position = from_behind(up_position, "space", 1)
    upper_position = from_behind(down_position, "space", -1)
    collide = pl.pallas_call(
        main_kernel,
        grid=(steps,),
        in_specs=[
            pl.BlockSpec((six, chunk, part), lambda i: (0, i, 0)),
            pl.BlockSpec((chunk, part), lambda i: (i, 0)),
            pl.BlockSpec((pairs, chunk), lambda i: (0, i)),
            pl.BlockSpec((pairs, chunk), lambda i: (0, i)),
            pl.BlockSpec((1, cap), lambda i: (0, 0)),
            pl.BlockSpec(memory_space=pltpu.SMEM),
            pl.BlockSpec((1, cap), lambda i: (0, 0)),
            pl.BlockSpec((2, cap), lambda i: (0, 0)),
        ],
        out_specs=[
            pl.BlockSpec((six, chunk, part), lambda i: (0, i + 1, 0)),
            pl.BlockSpec((three, MOVE, part), lambda i: (0, 0, 0)),
            pl.BlockSpec((three, MOVE, part), lambda i: (0, 0, 0)),
            pl.BlockSpec((reps, 4, share), lambda i: (0, 0, 0)),
        ],
        out_shape=[
            jax.ShapeDtypeStruct((six, out_cap, part), f32),
            parcel,
            parcel,
            jax.ShapeDtypeStruct((reps, 4, share), f32),
        ],
        scratch_shapes=[
            pltpu.VMEM((4, 8, part), f32),
            pltpu.VMEM((chunk, part), jnp.int32),
            pltpu.VMEM((chunk, part), f32),
            pltpu.VMEM((chunk, part), jnp.int32),
            pltpu.VMEM((3, cap, three * part), jnp.bfloat16),
            pltpu.VMEM((cap, part), f32),
        ],
        cost_estimate=pl.CostEstimate(flops=10 ** 9, bytes_accessed=8 * 10 ** 6, transcendentals=0),
        name="step",
    )
    operands = (
        current,
        pair_order.reshape(cap, part),
        jnp.transpose(accepted.reshape(cap, pairs)),
        jnp.transpose(direction.reshape(cap, pairs)),
        targets,
        live_count,
        cell_index.reshape(1, cap),
        slots,
    )
    moved, up_velocity, down_velocity, cell_terms = collide(*operands)
    lower_velocity = from_behind(up_velocity, "space", 1)
    upper_velocity = from_behind(down_velocity, "space", -1)
    total = cell_terms[0]
    for away in range(1, reps):
        total = total + from_behind(cell_terms[away], "rep", away)
    samples = (total / (part * reps))[:, None, :]
    for at, position, velocity in (
        (0, lower_position, lower_velocity),
        (MOVE + cap, upper_position, upper_velocity),
    ):
        arrived = jnp.concatenate([position + TIME_STEP * velocity, velocity], axis=0)
        moved = lax.dynamic_update_slice(moved, arrived, (0, at, 0))
    return (moved[:, None], samples)


def solution(mesh):
    return jax.shard_map(
        per_device,
        mesh=mesh,
        in_specs=(
            P(None, "rep", "space", None),
            P("rep", "space", None),
            P("rep", "space", None),
            P("rep", "space", None),
            P("rep", "space"),
            P("rep", "space"),
            P("rep", "space"),
        ),
        out_specs=(P(None, "rep", "space", None), P(None, "space", "rep")),
        check_vma=False,
    )
```

```python
import functools

import jax
import jax.numpy as jnp
from jax import lax
from jax.experimental import pallas as pl
from jax.experimental.pallas import tpu as pltpu
from jax.sharding import PartitionSpec as P

NDIR = 256
MOVE = 128
CELLS = 256
TIME_STEP = 0.25
GOLDEN_TURN = 2.399963229728653
ROWS = 128


def take_lanes(values, index):
    return jnp.take_along_axis(values, index, axis=1, mode="promise_in_bounds")


def split3(value):
    high = value.astype(jnp.bfloat16)
    rest = value - high.astype(jnp.float32)
    middle = rest.astype(jnp.bfloat16)
    low = (rest - middle.astype(jnp.float32)).astype(jnp.bfloat16)
    return high, middle, low


def dot(left, right):
    return jnp.dot(left, right, preferred_element_type=jnp.float32)


def dot_nt(left, right):
    return lax.dot_general(left, right, (((1,), (1,)), ((), ())), preferred_element_type=jnp.float32)


def inverse_order(order):
    chunk, part = order.shape
    count = part // 8
    lane = lax.broadcasted_iota(jnp.int32, (chunk, part), 1)
    keys = jnp.transpose((order * part + lane).astype(jnp.float32))
    rows = [keys[8 * i:8 * i + 8] for i in range(count)]
    sublane = lax.broadcasted_iota(jnp.int32, (8, chunk), 0)
    sign = None
    size = 2
    while size <= part:
        wanted = None
        if count <= size < part:
            wanted = jnp.where((sublane & (size // count)) == 0, 1.0, -1.0)
        if sign is not None or wanted is not None:
            flip = wanted if sign is None else sign if wanted is None else sign * wanted
            rows = [row * flip for row in rows]
        sign = wanted
        stride = size // 2
        while stride >= 1:
            if stride >= count:
                apart = stride // count
                is_low = (sublane & apart) == 0
                swapped = [jnp.take_along_axis(row, sublane ^ apart, axis=0, mode="promise_in_bounds") for row in rows]
                rows = [jnp.where(is_low, jnp.minimum(r, o), jnp.maximum(r, o)) for r, o in zip(rows, swapped)]
            else:
                after = list(rows)
                for i in range(count):
                    j = i ^ stride
                    rising = size >= count or (i & size) == 0
                    pick = jnp.minimum if (i < j) == rising else jnp.maximum
                    after[i] = pick(rows[i], rows[j])
                rows = after
            stride //= 2
        size *= 2
    ranked = [(row - ((sublane * count + i) * part).astype(jnp.float32)) for i, row in enumerate(rows)]
    placed = jnp.transpose(jnp.concatenate(ranked, axis=0)).astype(jnp.int32)
    return take_lanes(placed, (lane & (count - 1)) * 8 + lane // count)


def pick_rows(chosen, pieces):
    return dot(chosen, pieces[0]) + dot(chosen, pieces[1]) + dot(chosen, pieces[2])


def one_hot_rows(slots, cap):
    slot = lax.broadcasted_iota(jnp.int32, (MOVE, cap), 0)
    return jnp.concatenate(
        [jnp.where(slot == slots[j:j + 1, :], 1.0, 0.0) for j in range(2)], axis=0
    ).astype(jnp.bfloat16)


def mover_slots(dest, living, upper_slab, lower_slab):
    cap = dest.shape[1]
    chunk = MOVE
    leaving = [living & (dest == upper_slab), living & (dest == lower_slab)]
    flags = jnp.concatenate([jnp.where(m, 1.0, 0.0) for m in leaving], axis=0)
    triangle = (
        lax.broadcasted_iota(jnp.int32, (chunk, chunk), 0) <= lax.broadcasted_iota(jnp.int32, (chunk, chunk), 1)
    )
    triangle = jnp.where(triangle, 1.0, 0.0).astype(jnp.bfloat16)
    before = jnp.zeros((2, 1), jnp.float32)
    ranks = []
    for i in range(cap // chunk):
        piece = flags[:, i * chunk:(i + 1) * chunk]
        inside = dot(piece.astype(jnp.bfloat16), triangle)
        ranks.append(inside + before)
        before = before + inside[:, chunk - 1:chunk]
    ranking = jnp.concatenate(ranks, axis=1)
    return jnp.where(flags > 0.0, ranking - 1.0, -1.0).astype(jnp.int32)


def main_kernel(slabs, steps, part_ref, order_ref, flag_ref, turn_ref, dest_ref, live_ref, cell_ref, place_ref,
                moved_ref, samples_ref, table, packed_t, keep_t, inverse_t, parts, square, slot_ref,
                sent_place, sent_speed, got_place, got_speed, sent_cells, got_cells, send_sem, recv_sem):
    step = pl.program_id(0)
    chunk, part = order_ref.shape
    pairs = part // 2
    cap = dest_ref.shape[1]
    reps, _, share = sent_cells.shape
    my_slab = lax.axis_index("space")
    my_rep = lax.axis_index("rep")
    upper_slab = lax.rem(my_slab + 1, slabs)
    lower_slab = lax.rem(my_slab + slabs - 1, slabs)
    goals = (upper_slab, lower_slab)

    def copy(source, target, k, device):
        return pltpu.make_async_remote_copy(
            src_ref=source, dst_ref=target, send_sem=send_sem.at[k], recv_sem=recv_sem.at[k],
            device_id=device, device_id_type=pl.DeviceIdType.MESH,
        )

    place_copies, speed_copies = [
        [[copy(sent.at[j, k], got.at[j, k], base + 3 * j + k, {"space": goals[j]}) for k in range(3)] for j in range(2)]
        for sent, got, base in ((sent_place, got_place, 0), (sent_speed, got_speed, 6))
    ]
    cell_copies = [
        copy(sent_cells.at[k], got_cells.at[k], 11 + k, {"rep": lax.rem(my_rep + k, reps)}) for k in range(1, reps)
    ]

    @pl.when(step == 0)
    def _():
        barrier = pltpu.get_barrier_semaphore()
        for j in range(2):
            pl.semaphore_signal(barrier, inc=1, device_id={"space": goals[j]}, device_id_type=pl.DeviceIdType.MESH)
        for k in range(1, reps):
            pl.semaphore_signal(
                barrier, inc=1, device_id={"rep": lax.rem(my_rep + k, reps)}, device_id_type=pl.DeviceIdType.MESH
            )
        living = lax.broadcasted_iota(jnp.int32, (1, cap), 1) < live_ref[...]
        slots = mover_slots(dest_ref[...], living, upper_slab, lower_slab)
        slot_ref[...] = slots
        chosen = one_hot_rows(slots, cap)
        for k in range(3):
            sent = pick_rows(chosen, split3(place_ref[k]))
            sent_place[0, k] = sent[:MOVE]
            sent_place[1, k] = sent[MOVE:]
            if k == 0:
                pl.semaphore_wait(barrier, 1 + reps)
            for j in range(2):
                place_copies[j][k].start()

    @pl.when(step == 0)
    def _():
        for half in range(2):
            turns = (lax.broadcasted_iota(jnp.int32, (8, part), 1) + half * part).astype(jnp.float32)
            height = 1.0 - (2.0 * turns + 1.0) / NDIR
            radius = jnp.sqrt(1.0 - height * height)
            angle = turns * GOLDEN_TURN
            table[half] = radius * jnp.cos(angle)
            table[half + 2] = radius * jnp.sin(angle)

    @pl.when(step < steps)
    def _():
        pair_code = turn_ref[...] + NDIR * flag_ref[...]
        packed_t[...] = jnp.transpose(jnp.concatenate([pair_code, pair_code], axis=0))
        start = pl.multiple_of(step * chunk, chunk)
        slots = lax.broadcasted_iota(jnp.int32, (1, chunk), 1) + step * chunk
        staying = (dest_ref[:, pl.ds(start, chunk)] == my_slab) & (slots < live_ref[...])
        stay_rows = jnp.broadcast_to(jnp.where(staying, 1.0, 0.0), (part, chunk))
        keep_t[...] = jnp.transpose(stay_rows)
        inverse_t[...] = inverse_order(order_ref[...])

        def rows_step(i, carry):
            row = pl.multiple_of(i * ROWS, ROWS)
            here = pl.ds(row, ROWS)
            order = order_ref[here, :]
            inverse = inverse_t[here, :]
            partner = take_lanes(order, inverse ^ pairs)
            code = take_lanes(packed_t[here, :], inverse & (pairs - 1))
            taken = code >= NDIR
            turn = code & (NDIR - 1)
            low_index = turn & (part - 1)
            is_high = turn >= part
            wide = (ROWS, part)
            tables = [jnp.broadcast_to(table[k, 0:1, :], wide) for k in range(4)]
            unit_x = jnp.where(is_high, take_lanes(tables[1], low_index), take_lanes(tables[0], low_index))
            unit_y = jnp.where(is_high, take_lanes(tables[3], low_index), take_lanes(tables[2], low_index))
            unit_z = 1.0 - (2.0 * turn.astype(jnp.float32) + 1.0) / NDIR
            old = [part_ref[3 + k, here, :] for k in range(3)]
            other = [take_lanes(v, partner) for v in old]
            relative = [a - b for a, b in zip(old, other)]
            speed = jnp.sqrt(relative[0] * relative[0] + relative[1] * relative[1] + relative[2] * relative[2])
            half_speed = jnp.where(inverse < pairs, 0.5, -0.5) * speed
            new = [
                jnp.where(taken, 0.5 * (a + b) + half_speed * u, a)
                for a, b, u in zip(old, other, (unit_x, unit_y, unit_z))
            ]
            keep = keep_t[here, :] > 0.0
            target = pl.ds(pl.multiple_of(MOVE + step * chunk + row, ROWS), ROWS)
            block = pl.ds(pl.multiple_of(step * chunk + row, ROWS), ROWS)
            square[block, :] = new[0] * new[0] + new[1] * new[1] + new[2] * new[2]
            for k in range(3):
                moved_ref[k, target, :] = jnp.where(keep, part_ref[k, here, :] + TIME_STEP * new[k], 0.0)
                moved_ref[3 + k, target, :] = jnp.where(keep, new[k], 0.0)
                for j, piece in enumerate(split3(new[k])):
                    parts[j, block, pl.ds(k * part, part)] = piece
            return carry

        lax.fori_loop(0, chunk // ROWS, rows_step, 0)

    @pl.when(step == steps - 1)
    def _():
        chosen = one_hot_rows(slot_ref[...], cap)
        for k in range(3):
            sent = pick_rows(chosen, [parts[j, :, pl.ds(k * part, part)] for j in range(3)])
            sent_speed[0, k] = sent[:MOVE]
            sent_speed[1, k] = sent[MOVE:]
            for j in range(2):
                speed_copies[j][k].start()

        living = lax.broadcasted_iota(jnp.int32, (1, cap), 1) < live_ref[...]
        ones = jnp.ones((8, part), jnp.bfloat16)
        eight = lax.broadcasted_iota(jnp.int32, (8, cap), 0)
        terms = []
        for k in range(3):
            here = pl.ds(k * part, part)
            terms.append(dot_nt(ones, parts[0, :, here]) + dot_nt(ones, parts[1, :, here]) + dot_nt(ones, parts[2, :, here]))
        pieces = split3(square[...])
        terms.append(dot_nt(ones, pieces[0]) + dot_nt(ones, pieces[1]) + dot_nt(ones, pieces[2]))
        term = jnp.where(eight == 0, terms[0], jnp.where(eight == 1, terms[1], jnp.where(eight == 2, terms[2], terms[3])))
        term = jnp.where(living, term, 0.0)
        shifted = cell_ref[...] + (CELLS - my_rep * share)
        shifted = jnp.where(shifted >= CELLS, shifted - CELLS, shifted)
        cells = lax.broadcasted_iota(jnp.int32, (CELLS, cap), 0)
        in_cell = jnp.where(cells == shifted, 1.0, 0.0).astype(jnp.bfloat16)
        high, middle, low = split3(term)
        total = dot_nt(high, in_cell) + dot_nt(middle, in_cell) + dot_nt(low, in_cell)
        for j in range(reps):
            sent_cells[j] = total[0:4, j * share:(j + 1) * share]
        for each in cell_copies:
            each.start()

        total = sent_cells[0]
        for k in range(1, reps):
            cell_copies[k - 1].wait()
            total = total + got_cells[k]
        samples_ref[...] = total / (part * reps)
        for k in range(3):
            for j, at in ((0, 0), (1, MOVE + cap)):
                target = pl.ds(at, MOVE)
                place_copies[j][k].wait()
                speed_copies[j][k].wait()
                moved_ref[k, target, :] = got_place[j, k] + TIME_STEP * got_speed[j, k]
                moved_ref[3 + k, target, :] = got_speed[j, k]


def per_device(particles, pair_order, accepted, direction, destination, live_count, cell_index):
    six, _, cap, part = particles.shape
    three = six // 2
    pairs = accepted.shape[2]
    chunk = MOVE
    steps = cap // chunk
    slabs = lax.axis_size("space")
    reps = lax.axis_size("rep")
    share = CELLS // reps
    f32 = jnp.float32
    out_cap = cap + 2 * MOVE
    current = particles.reshape(six, cap, part)
    call = pl.pallas_call(
        functools.partial(main_kernel, slabs, steps),
        grid=(steps,),
        in_specs=[
            pl.BlockSpec((six, chunk, part), lambda i: (0, i, 0)),
            pl.BlockSpec((chunk, part), lambda i: (i, 0)),
            pl.BlockSpec((pairs, chunk), lambda i: (0, i)),
            pl.BlockSpec((pairs, chunk), lambda i: (0, i)),
            pl.BlockSpec((1, cap), lambda i: (0, 0)),
            pl.BlockSpec((1, 1), lambda i: (0, 0)),
            pl.BlockSpec((1, cap), lambda i: (0, 0)),
            pl.BlockSpec((three, cap, part), lambda i: (0, 0, 0)),
        ],
        out_specs=[
            pl.BlockSpec(memory_space=pltpu.VMEM),
            pl.BlockSpec((4, share), lambda i: (0, 0)),
        ],
        out_shape=[
            jax.ShapeDtypeStruct((six, out_cap, part), f32),
            jax.ShapeDtypeStruct((4, share), f32),
        ],
        scratch_shapes=[
            pltpu.VMEM((4, 8, part), f32),
            pltpu.VMEM((chunk, part), jnp.int32),
            pltpu.VMEM((chunk, part), f32),
            pltpu.VMEM((chunk, part), jnp.int32),
            pltpu.VMEM((3, cap, three * part), jnp.bfloat16),
            pltpu.VMEM((cap, part), f32),
            pltpu.VMEM((2, cap), jnp.int32),
            pltpu.VMEM((2, three, MOVE, part), f32),
            pltpu.VMEM((2, three, MOVE, part), f32),
            pltpu.VMEM((2, three, MOVE, part), f32),
            pltpu.VMEM((2, three, MOVE, part), f32),
            pltpu.VMEM((reps, 4, share), f32),
            pltpu.VMEM((reps, 4, share), f32),
            pltpu.SemaphoreType.DMA((11 + reps,)),
            pltpu.SemaphoreType.DMA((11 + reps,)),
        ],
        compiler_params=pltpu.CompilerParams(collective_id=0, has_side_effects=True, vmem_limit_bytes=16 * 2 ** 20),
        name="step",
    )
    operands = (
        current,
        pair_order.reshape(cap, part),
        jnp.transpose(accepted.reshape(cap, pairs)),
        jnp.transpose(direction.reshape(cap, pairs)),
        destination.reshape(1, cap),
        live_count,
        cell_index.reshape(1, cap),
        current,
    )
    hold = functools.partial(pltpu.with_memory_space_constraint, memory_space=pltpu.HBM)
    operands = [x if x is live_count else hold(x) for x in operands]
    moved, samples = call(*operands)
    return (moved[:, None], samples[:, None, :])


def solution(mesh):
    return jax.shard_map(
        per_device,
        mesh=mesh,
        in_specs=(
            P(None, "rep", "space", None),
            P("rep", "space", None),
            P("rep", "space", None),
            P("rep", "space", None),
            P("rep", "space"),
            P("rep", "space"),
            P("rep", "space"),
        ),
        out_specs=(P(None, "rep", "space", None), P(None, "space", "rep")),
        check_vma=False,
    )
```

```python
import functools

import jax
import jax.numpy as jnp
from jax import lax
from jax.experimental import pallas as pl
from jax.experimental.pallas import tpu as pltpu
from jax.sharding import PartitionSpec as P

NDIR = 256
MOVE = 128
CELLS = 256
TIME_STEP = 0.25
GOLDEN_TURN = 2.399963229728653
ROWS = 128


def take_lanes(values, index):
    return jnp.take_along_axis(values, index, axis=1, mode="promise_in_bounds")


def split3(value):
    high = value.astype(jnp.bfloat16)
    rest = value - high.astype(jnp.float32)
    middle = rest.astype(jnp.bfloat16)
    low = (rest - middle.astype(jnp.float32)).astype(jnp.bfloat16)
    return high, middle, low


def dot(left, right):
    return jnp.dot(left, right, preferred_element_type=jnp.float32)


def dot_nt(left, right):
    return lax.dot_general(left, right, (((1,), (1,)), ((), ())), preferred_element_type=jnp.float32)


def inverse_order(order):
    chunk, part = order.shape
    count = part // 8
    lane = lax.broadcasted_iota(jnp.int32, (chunk, part), 1)
    keys = jnp.transpose((order * part + lane).astype(jnp.float32))
    rows = [keys[8 * i:8 * i + 8] for i in range(count)]
    sublane = lax.broadcasted_iota(jnp.int32, (8, chunk), 0)
    sign = None
    size = 2
    while size <= part:
        wanted = None
        if count <= size < part:
            wanted = jnp.where((sublane & (size // count)) == 0, 1.0, -1.0)
        if sign is not None or wanted is not None:
            flip = wanted if sign is None else sign if wanted is None else sign * wanted
            rows = [row * flip for row in rows]
        sign = wanted
        stride = size // 2
        while stride >= 1:
            if stride >= count:
                apart = stride // count
                is_low = (sublane & apart) == 0
                swapped = [jnp.take_along_axis(row, sublane ^ apart, axis=0, mode="promise_in_bounds") for row in rows]
                rows = [jnp.where(is_low, jnp.minimum(r, o), jnp.maximum(r, o)) for r, o in zip(rows, swapped)]
            else:
                after = list(rows)
                for i in range(count):
                    j = i ^ stride
                    rising = size >= count or (i & size) == 0
                    pick = jnp.minimum if (i < j) == rising else jnp.maximum
                    after[i] = pick(rows[i], rows[j])
                rows = after
            stride //= 2
        size *= 2
    ranked = [(row - ((sublane * count + i) * part).astype(jnp.float32)) for i, row in enumerate(rows)]
    placed = jnp.transpose(jnp.concatenate(ranked, axis=0)).astype(jnp.int32)
    return take_lanes(placed, (lane & (count - 1)) * 8 + lane // count)


def pick_rows(chosen, pieces):
    return dot(chosen, pieces[0]) + dot(chosen, pieces[1]) + dot(chosen, pieces[2])


def one_hot_rows(slots, cap):
    slot = lax.broadcasted_iota(jnp.int32, (MOVE, cap), 0)
    return jnp.concatenate(
        [jnp.where(slot == slots[j:j + 1, :], 1.0, 0.0) for j in range(2)], axis=0
    ).astype(jnp.bfloat16)


def mover_slots(dest, living, upper_slab, lower_slab):
    cap = dest.shape[1]
    chunk = MOVE
    leaving = [living & (dest == upper_slab), living & (dest == lower_slab)]
    flags = jnp.concatenate([jnp.where(m, 1.0, 0.0) for m in leaving], axis=0)
    triangle = (
        lax.broadcasted_iota(jnp.int32, (chunk, chunk), 0) <= lax.broadcasted_iota(jnp.int32, (chunk, chunk), 1)
    )
    triangle = jnp.where(triangle, 1.0, 0.0).astype(jnp.bfloat16)
    before = jnp.zeros((2, 1), jnp.float32)
    ranks = []
    for i in range(cap // chunk):
        piece = flags[:, i * chunk:(i + 1) * chunk]
        inside = dot(piece.astype(jnp.bfloat16), triangle)
        ranks.append(inside + before)
        before = before + inside[:, chunk - 1:chunk]
    ranking = jnp.concatenate(ranks, axis=1)
    return jnp.where(flags > 0.0, ranking - 1.0, -1.0).astype(jnp.int32)


def main_kernel(slabs, steps, part_ref, order_ref, flag_ref, turn_ref, dest_ref, live_ref, cell_ref, place_ref,
                moved_ref, samples_ref, table, packed_t, keep_t, inverse_t, parts, square, slot_ref,
                sent_place, sent_speed, got_place, got_speed, sent_cells, got_cells, send_sem, recv_sem, places, load_sem):
    step = pl.program_id(0)
    chunk, part = order_ref.shape
    pairs = part // 2
    cap = dest_ref.shape[1]
    reps, _, share = sent_cells.shape
    my_slab = lax.axis_index("space")
    my_rep = lax.axis_index("rep")
    upper_slab = lax.rem(my_slab + 1, slabs)
    lower_slab = lax.rem(my_slab + slabs - 1, slabs)
    goals = (upper_slab, lower_slab)

    def copy(source, target, k, device):
        return pltpu.make_async_remote_copy(
            src_ref=source, dst_ref=target, send_sem=send_sem.at[k], recv_sem=recv_sem.at[k],
            device_id=device, device_id_type=pl.DeviceIdType.MESH,
        )

    place_copies, speed_copies = [
        [[copy(sent.at[j, k], got.at[j, k], base + 3 * j + k, {"space": goals[j]}) for k in range(3)] for j in range(2)]
        for sent, got, base in ((sent_place, got_place, 0), (sent_speed, got_speed, 6))
    ]
    cell_copies = [
        copy(sent_cells.at[k], got_cells.at[k], 11 + k, {"rep": lax.rem(my_rep + k, reps)}) for k in range(1, reps)
    ]

    @pl.when(step == 0)
    def _():
        barrier = pltpu.get_barrier_semaphore()
        for j in range(2):
            pl.semaphore_signal(barrier, inc=1, device_id={"space": goals[j]}, device_id_type=pl.DeviceIdType.MESH)
        for k in range(1, reps):
            pl.semaphore_signal(
                barrier, inc=1, device_id={"rep": lax.rem(my_rep + k, reps)}, device_id_type=pl.DeviceIdType.MESH
            )
        load = pltpu.make_async_copy(place_ref.at[pl.ds(0, 3)], places, load_sem)
        load.start()
        living = lax.broadcasted_iota(jnp.int32, (1, cap), 1) < live_ref[...]
        slots = mover_slots(dest_ref[...], living, upper_slab, lower_slab)
        slot_ref[...] = slots
        chosen = one_hot_rows(slots, cap)
        load.wait()
        for k in range(3):
            sent = pick_rows(chosen, split3(places[k]))
            sent_place[0, k] = sent[:MOVE]
            sent_place[1, k] = sent[MOVE:]
            if k == 0:
                pl.semaphore_wait(barrier, 1 + reps)
            for j in range(2):
                place_copies[j][k].start()

    @pl.when(step == 0)
    def _():
        for half in range(2):
            turns = (lax.broadcasted_iota(jnp.int32, (8, part), 1) + half * part).astype(jnp.float32)
            height = 1.0 - (2.0 * turns + 1.0) / NDIR
            radius = jnp.sqrt(1.0 - height * height)
            angle = turns * GOLDEN_TURN
            table[half] = radius * jnp.cos(angle)
            table[half + 2] = radius * jnp.sin(angle)

    @pl.when(step < steps)
    def _():
        pair_code = turn_ref[...] + NDIR * flag_ref[...]
        packed_t[...] = jnp.transpose(jnp.concatenate([pair_code, pair_code], axis=0))
        start = pl.multiple_of(step * chunk, chunk)
        slots = lax.broadcasted_iota(jnp.int32, (1, chunk), 1) + step * chunk
        staying = (dest_ref[:, pl.ds(start, chunk)] == my_slab) & (slots < live_ref[...])
        stay_rows = jnp.broadcast_to(jnp.where(staying, 1.0, 0.0), (part, chunk))
        keep_t[...] = jnp.transpose(stay_rows)
        inverse_t[...] = inverse_order(order_ref[...])

        def rows_step(i, carry):
            row = pl.multiple_of(i * ROWS, ROWS)
            here = pl.ds(row, ROWS)
            order = order_ref[here, :]
            inverse = inverse_t[here, :]
            partner = take_lanes(order, inverse ^ pairs)
            code = take_lanes(packed_t[here, :], inverse & (pairs - 1))
            taken = code >= NDIR
            turn = code & (NDIR - 1)
            low_index = turn & (part - 1)
            is_high = turn >= part
            wide = (ROWS, part)
            tables = [jnp.broadcast_to(table[k, 0:1, :], wide) for k in range(4)]
            unit_x = jnp.where(is_high, take_lanes(tables[1], low_index), take_lanes(tables[0], low_index))
            unit_y = jnp.where(is_high, take_lanes(tables[3], low_index), take_lanes(tables[2], low_index))
            unit_z = 1.0 - (2.0 * turn.astype(jnp.float32) + 1.0) / NDIR
            old = [part_ref[3 + k, here, :] for k in range(3)]
            other = [take_lanes(v, partner) for v in old]
            relative = [a - b for a, b in zip(old, other)]
            speed = jnp.sqrt(relative[0] * relative[0] + relative[1] * relative[1] + relative[2] * relative[2])
            half_speed = jnp.where(inverse < pairs, 0.5, -0.5) * speed
            new = [
                jnp.where(taken, 0.5 * (a + b) + half_speed * u, a)
                for a, b, u in zip(old, other, (unit_x, unit_y, unit_z))
            ]
            keep = keep_t[here, :] > 0.0
            target = pl.ds(pl.multiple_of(MOVE + step * chunk + row, ROWS), ROWS)
            block = pl.ds(pl.multiple_of(step * chunk + row, ROWS), ROWS)
            square[block, :] = new[0] * new[0] + new[1] * new[1] + new[2] * new[2]
            for k in range(3):
                moved_ref[k, target, :] = jnp.where(keep, part_ref[k, here, :] + TIME_STEP * new[k], 0.0)
                moved_ref[3 + k, target, :] = jnp.where(keep, new[k], 0.0)
                for j, piece in enumerate(split3(new[k])):
                    parts[j, block, pl.ds(k * part, part)] = piece
            return carry

        lax.fori_loop(0, chunk // ROWS, rows_step, 0)

    @pl.when(step == steps - 1)
    def _():
        chosen = one_hot_rows(slot_ref[...], cap)
        for k in range(3):
            sent = pick_rows(chosen, [parts[j, :, pl.ds(k * part, part)] for j in range(3)])
            sent_speed[0, k] = sent[:MOVE]
            sent_speed[1, k] = sent[MOVE:]
            for j in range(2):
                speed_copies[j][k].start()

        living = lax.broadcasted_iota(jnp.int32, (1, cap), 1) < live_ref[...]
        ones = jnp.ones((8, part), jnp.bfloat16)
        eight = lax.broadcasted_iota(jnp.int32, (8, cap), 0)
        terms = []
        for k in range(3):
            here = pl.ds(k * part, part)
            terms.append(dot_nt(ones, parts[0, :, here]) + dot_nt(ones, parts[1, :, here]) + dot_nt(ones, parts[2, :, here]))
        pieces = split3(square[...])
        terms.append(dot_nt(ones, pieces[0]) + dot_nt(ones, pieces[1]) + dot_nt(ones, pieces[2]))
        term = jnp.where(eight == 0, terms[0], jnp.where(eight == 1, terms[1], jnp.where(eight == 2, terms[2], terms[3])))
        term = jnp.where(living, term, 0.0)
        shifted = cell_ref[...] + (CELLS - my_rep * share)
        shifted = jnp.where(shifted >= CELLS, shifted - CELLS, shifted)
        cells = lax.broadcasted_iota(jnp.int32, (CELLS, cap), 0)
        in_cell = jnp.where(cells == shifted, 1.0, 0.0).astype(jnp.bfloat16)
        high, middle, low = split3(term)
        total = dot_nt(high, in_cell) + dot_nt(middle, in_cell) + dot_nt(low, in_cell)
        for j in range(reps):
            sent_cells[j] = total[0:4, j * share:(j + 1) * share]
        for each in cell_copies:
            each.start()

        total = sent_cells[0]
        for k in range(1, reps):
            cell_copies[k - 1].wait()
            total = total + got_cells[k]
        total = total / (part * reps)
        for k in range(4):
            samples_ref[k] = total[k:k + 1]
        for k in range(3):
            for j, at in ((0, 0), (1, MOVE + cap)):
                target = pl.ds(at, MOVE)
                place_copies[j][k].wait()
                speed_copies[j][k].wait()
                moved_ref[k, target, :] = got_place[j, k] + TIME_STEP * got_speed[j, k]
                moved_ref[3 + k, target, :] = got_speed[j, k]


def per_device(particles, pair_order, accepted, direction, destination, live_count, cell_index):
    six, _, cap, part = particles.shape
    three = six // 2
    pairs = accepted.shape[2]
    chunk = MOVE
    steps = cap // chunk
    slabs = lax.axis_size("space")
    reps = lax.axis_size("rep")
    share = CELLS // reps
    f32 = jnp.float32
    out_cap = cap + 2 * MOVE
    current = particles.reshape(six, cap, part)
    call = pl.pallas_call(
        functools.partial(main_kernel, slabs, steps),
        grid=(steps,),
        in_specs=[
            pl.BlockSpec((six, chunk, part), lambda i: (0, i, 0)),
            pl.BlockSpec((chunk, part), lambda i: (i, 0)),
            pl.BlockSpec((pairs, chunk), lambda i: (0, i)),
            pl.BlockSpec((pairs, chunk), lambda i: (0, i)),
            pl.BlockSpec((1, cap), lambda i: (0, 0)),
            pl.BlockSpec((1, 1), lambda i: (0, 0)),
            pl.BlockSpec((1, cap), lambda i: (0, 0)),
            pl.BlockSpec(memory_space=pltpu.HBM),
        ],
        out_specs=[
            pl.BlockSpec(memory_space=pltpu.VMEM),
            pl.BlockSpec((4, 1, share), lambda i: (0, 0, 0)),
        ],
        out_shape=[
            jax.ShapeDtypeStruct((six, out_cap, part), f32),
            jax.ShapeDtypeStruct((4, 1, share), f32),
        ],
        scratch_shapes=[
            pltpu.VMEM((4, 8, part), f32),
            pltpu.VMEM((chunk, part), jnp.int32),
            pltpu.VMEM((chunk, part), f32),
            pltpu.VMEM((chunk, part), jnp.int32),
            pltpu.VMEM((3, cap, three * part), jnp.bfloat16),
            pltpu.VMEM((cap, part), f32),
            pltpu.VMEM((2, cap), jnp.int32),
            pltpu.VMEM((2, three, MOVE, part), f32),
            pltpu.VMEM((2, three, MOVE, part), f32),
            pltpu.VMEM((2, three, MOVE, part), f32),
            pltpu.VMEM((2, three, MOVE, part), f32),
            pltpu.VMEM((reps, 4, share), f32),
            pltpu.VMEM((reps, 4, share), f32),
            pltpu.SemaphoreType.DMA((11 + reps,)),
            pltpu.SemaphoreType.DMA((11 + reps,)),
            pltpu.VMEM((three, cap, part), f32),
            pltpu.SemaphoreType.DMA,
        ],
        compiler_params=pltpu.CompilerParams(collective_id=0, has_side_effects=True, vmem_limit_bytes=16 * 2 ** 20),
        name="step",
    )
    operands = (
        current,
        pair_order.reshape(cap, part),
        jnp.transpose(accepted.reshape(cap, pairs)),
        jnp.transpose(direction.reshape(cap, pairs)),
        destination.reshape(1, cap),
        live_count,
        cell_index.reshape(1, cap),
        current,
    )
    hold = functools.partial(pltpu.with_memory_space_constraint, memory_space=pltpu.HBM)
    operands = [x if x is live_count else hold(x) for x in operands]
    moved, samples = call(*operands)
    return (moved[:, None], samples)


def solution(mesh):
    return jax.shard_map(
        per_device,
        mesh=mesh,
        in_specs=(
            P(None, "rep", "space", None),
            P("rep", "space", None),
            P("rep", "space", None),
            P("rep", "space", None),
            P("rep", "space"),
            P("rep", "space"),
            P("rep", "space"),
        ),
        out_specs=(P(None, "rep", "space", None), P(None, "space", "rep")),
        check_vma=False,
    )
```
